128 devices in a mesh: det: 16 (over z, y_hi, core), band: 8 (over y_lo, x).
Axes of the slice: x: 4, y: 4 (y_hi: 2, y_lo: 2; y = y_hi * 2 + y_lo), z: 4, core: 2. Of those that a mesh axis runs over, the one named last changes fastest.
Arguments:
- scan_lines: float32 [1024, 4096], P(('det', 'band')), may hold values from -6 to 6
- response: float32 [1024, 4096], P(('det', 'band')), may hold values from 0.02 to 1
- cycle_offset: int32 [1024, 4096], P(('det', 'band')), may hold values from 0 to 127
- column: int32 [1024, 4096], P(('det', 'band')), may hold values from 0 to 2047
- order_slot: int32 [256], replicated, may hold values from 0 to 255, each once
- legendre: float32 [256, 1024, 1024], P('det', 'band'), may hold values from -0.046875 to 0.046875
Outputs:
- harmonics: float32 [2, 256, 1024], P(None, 'det', 'band')
- sky_map: float32 [1024, 2048], P(('band', 'det'))
The draws below stay inside these ranges and needn't reach their ends.
Inputs may be any that keep to these rules, and one draw needn't show every extreme that they name: `order_slot`: each of the orders 0 to 255 stands in exactly one slot.
All inputs are finite; a program needn't handle non-finite values.
Results may differ from the reference program's by a relative error of at most 0.000073.
Values sent between devices are 32-bit elements; how exact they have to be, the bound alone decides.
A program may use at most 64 MiB of HBM per device.

```python
import math
import jax
import jax.numpy as jnp
import numpy as np
from jax import lax

S = 4096
NRING = 1024
NPHI = 2048
MMAX = 256
LMAX = 1024
DET_DEV = 8
DETS = 1024
RB = 128
N_BAND = 8


def with_ends(entries, own_key, smallest, top_value):
    longest = entries.shape.index(max(entries.shape))
    spots = []
    for shift in (0, 1):
        where = [jax.random.randint(jax.random.fold_in(own_key, axis), (), 0, length) for axis, length in enumerate(entries.shape)]
        where[longest] = (where[longest] + shift) % entries.shape[longest]
        spots.append(tuple(where))
    return entries.at[spots[0]].set(smallest).at[spots[1]].set(top_value)


def shard_levels(stream_key, shape, shards, smallest, high):
    def one(dim, parts):
        heights = jax.random.uniform(jax.random.fold_in(jax.random.fold_in(stream_key, 6), dim), (parts,), jnp.float32, smallest / len(shards), high / len(shards))
        return jnp.repeat(jnp.exp(heights), shape[dim] // parts).reshape((-1,) + (1,) * (len(shape) - dim - 1))

    level = one(*shards[0])
    for cut in shards[1:]:
        level = level * one(*cut)
    return level


def rank_bounds(count, slope):
    portions = [(1 << 20) // math.isqrt(rank ** slope) + 1 for rank in range(1, count + 1)]
    spread = 1 + sum(portions) // (1 << 30)
    return np.cumsum(np.array([max(1, weight // spread) for weight in portions]))


def ranked(own_key, extent, number_of, skew):
    listing = rank_bounds(number_of, skew)
    lot = jax.random.randint(jax.random.fold_in(own_key, 1), extent, 0, int(listing[number_of - 1]))
    grade = jnp.searchsorted(jnp.asarray(listing, jnp.int32), lot, side="right")
    return jax.random.permutation(jax.random.fold_in(own_key, 2), number_of)[grade].astype(jnp.int32)


def noise(stream_key, shape, scale, limit, split=(), kind=jnp.bfloat16):
    factor_of = shard_levels(stream_key, shape, split, -0.22, 0.18) if split else 1.0
    drawn = jax.random.normal(stream_key, shape, jnp.float32) * scale * factor_of
    return jnp.minimum(jnp.maximum(drawn, -limit), limit).astype(kind)


def setup_inputs(seed: int = 0) -> dict:
    seeds = jax.random.split(jax.random.key(seed), 7)
    scan_lines = noise(seeds[0], (DETS, S), 1.0, 6.0, ((0, 128),), jnp.float32)
    response = jnp.clip(jnp.exp(math.log(1.0) - 3.912023 * jax.random.uniform(seeds[1], (DETS, S), jnp.float32) ** shard_levels(seeds[1], (DETS, S), ((0, 128),), -0.2, 0.2)), 0.02, 1.0)
    cycle_offset = with_ends(jax.random.randint(seeds[2], (DETS, S), 0, RB), jax.random.fold_in(seeds[2], 1), 0, RB - 1).astype(jnp.int32)
    column = with_ends(ranked(seeds[3], (DETS, S), NPHI, 2), jax.random.fold_in(seeds[3], 3), 0, NPHI - 1).astype(jnp.int32)
    order_slot = jax.random.permutation(seeds[4], MMAX).astype(jnp.int32)
    legendre = noise(seeds[5], (MMAX, NRING, LMAX), (16 * NRING) ** -0.5, 0.046875, ((0, 16), (1, 8)), jnp.float32)
    return {"scan_lines": scan_lines, "response": response, "cycle_offset": cycle_offset, "column": column, "order_slot": order_slot, "legendre": legendre}


def reference(scan_lines, response, cycle_offset, column, order_slot, legendre):
    spectrum = jnp.fft.fft(scan_lines, axis=1) * response
    filtered = jnp.real(jnp.fft.ifft(spectrum, axis=1)).astype(jnp.float32)
    line_count = scan_lines.shape[0]
    band_cycles = NRING // N_BAND
    line_band = (jnp.arange(line_count, dtype=jnp.int32) // DET_DEV) % N_BAND
    cycle_index = line_band[:, None] * band_cycles + cycle_offset
    flat_index = (cycle_index * NPHI + column).reshape(-1)
    summed = jnp.zeros((NRING * NPHI,), jnp.float32).at[flat_index].add(filtered.reshape(-1))
    counts = jnp.zeros((NRING * NPHI,), jnp.float32).at[flat_index].add(1.0)
    sky_map = (summed / jnp.maximum(counts, 1.0)).reshape(NRING, NPHI)
    pixel_index = jnp.arange(NPHI, dtype=jnp.int32)[:, None]
    phases = (2.0 * jnp.pi / NPHI) * ((pixel_index * order_slot[None, :]) % NPHI).astype(jnp.float32)
    cycle_real = jnp.dot(sky_map, jnp.cos(phases), precision=lax.Precision.HIGHEST, preferred_element_type=jnp.float32)
    cycle_imag = -jnp.dot(sky_map, jnp.sin(phases), precision=lax.Precision.HIGHEST, preferred_element_type=jnp.float32)
    cycle_modes = jnp.stack([cycle_real, cycle_imag])
    degree_index = jnp.arange(LMAX, dtype=jnp.int32)
    keep_mask = (degree_index[None, :] >= order_slot[:, None]).astype(jnp.float32)
    harmonics = jnp.einsum("crs,srl->csl", cycle_modes, legendre, precision=lax.Precision.HIGHEST) * keep_mask[None]
    return harmonics, sky_map
```

```python
import functools

import jax
import jax.numpy as jnp
from jax import lax
from jax.experimental import pallas as pl
from jax.experimental.pallas import tpu as pltpu
from jax.sharding import PartitionSpec as P

NPHI = 2048
LMAX = 1024


precise = lax.Precision.HIGHEST


def cut_along(x, dim, count):
    before, after = (x.shape[:dim], x.shape[dim + 1 :])
    return jnp.moveaxis(x.reshape(*before, count, -1, *after), dim, 0)


def summed_on_arrival(x, axis, dim):
    count = lax.axis_size(axis)
    blocks = lax.all_to_all(cut_along(x, dim, count), axis, 0, 0, tiled=True)
    return jnp.sum(blocks, axis=0)


def side_by_side(arrays, axis, dim, along):
    widths = [a.shape[along] for a in arrays]
    both = jnp.concatenate(arrays, axis=along)
    whole = summed_on_arrival(both, axis, dim)
    return tuple(jnp.split(whole, [sum(widths[:k]) for k in range(1, len(widths))], axis=along))


def twiddle_pair(count_rows, count_cols, modulus):
    row_index = jnp.arange(count_rows, dtype=jnp.int32)[:, None]
    col_index = jnp.arange(count_cols, dtype=jnp.int32)[None, :]
    phases = 2.0 * jnp.pi / modulus * (row_index * col_index % modulus).astype(jnp.float32)
    return (jnp.cos(phases), jnp.sin(phases))


def noise_filter(scan_lines, response):
    line_count, length = scan_lines.shape
    log_size = length.bit_length() - 1
    inner_len = 1 << log_size // 2
    outer_len = length // inner_len
    cos_outer, sin_outer = twiddle_pair(outer_len, outer_len, outer_len)
    cos_inner, sin_inner = twiddle_pair(inner_len, inner_len, inner_len)
    twist_cos, twist_sin = twiddle_pair(outer_len, inner_len, length)
    shaped = scan_lines.reshape(line_count, outer_len, inner_len)
    first_real = jnp.einsum("lna,nk->lka", shaped, cos_outer, precision=precise)
    first_imag = -jnp.einsum("lna,nk->lka", shaped, sin_outer, precision=precise)
    turned_real = first_real * twist_cos + first_imag * twist_sin
    turned_imag = first_imag * twist_cos - first_real * twist_sin
    spec_real = jnp.einsum("lka,aj->lkj", turned_real, cos_inner, precision=precise) + jnp.einsum(
        "lka,aj->lkj", turned_imag, sin_inner, precision=precise
    )
    spec_imag = jnp.einsum("lka,aj->lkj", turned_imag, cos_inner, precision=precise) - jnp.einsum(
        "lka,aj->lkj", turned_real, sin_inner, precision=precise
    )
    weights_k = response.reshape(line_count, inner_len, outer_len).transpose(0, 2, 1)
    spec_real = spec_real * weights_k
    spec_imag = spec_imag * weights_k
    back_real = jnp.einsum("lkj,jn->lkn", spec_real, cos_inner, precision=precise) - jnp.einsum(
        "lkj,jn->lkn", spec_imag, sin_inner, precision=precise
    )
    back_imag = jnp.einsum("lkj,jn->lkn", spec_imag, cos_inner, precision=precise) + jnp.einsum(
        "lkj,jn->lkn", spec_real, sin_inner, precision=precise
    )
    untwist_real = back_real * twist_cos - back_imag * twist_sin
    untwist_imag = back_imag * twist_cos + back_real * twist_sin
    result = jnp.einsum("lkn,km->lmn", untwist_real, cos_outer, precision=precise) - jnp.einsum(
        "lkn,km->lmn", untwist_imag, sin_outer, precision=precise
    )
    return (result / length).reshape(line_count, length)


def one_hot(index, count):
    own = lax.broadcasted_iota(jnp.int32, (count, index.shape[1]), 0)
    wide = jnp.broadcast_to(index.astype(jnp.float32), own.shape)
    return wide.astype(jnp.bfloat16) == own.astype(jnp.float32).astype(jnp.bfloat16)


def bin_kernel(cycles, block, value_ref, cycle_ref, column_ref, out_ref):
    lines, length = value_ref.shape
    out_ref[...] = jnp.zeros_like(out_ref)
    steps = length // block
    zero, one = jnp.bfloat16(0), jnp.bfloat16(1)

    def step(t, carry):
        line, start = t // steps, pl.multiple_of(t % steps * block, block)
        where = (pl.ds(line, 1), pl.ds(start, block))
        value, cycle, column = value_ref[where], cycle_ref[where], column_ref[where]
        high = value.astype(jnp.bfloat16).astype(jnp.float32)
        low = value - high
        hit = one_hot(cycle, cycles)
        spread = lambda x: jnp.where(hit, jnp.broadcast_to(x, hit.shape).astype(jnp.bfloat16), zero)
        rows = jnp.concatenate([spread(high), spread(low), jnp.where(hit, one, zero)], 0)
        cols = jnp.concatenate(
            [jnp.where(one_hot(column - n, 256), one, zero) for n in range(0, NPHI, 256)], 0
        )
        out_ref[...] += lax.dot_general(
            rows, cols, (((1,), (1,)), ((), ())), preferred_element_type=jnp.float32
        )
        return carry

    lax.fori_loop(0, lines * steps, step, 0)


def bin_samples(value, cycle, column, cycles):
    out = pl.pallas_call(
        functools.partial(bin_kernel, cycles, 1024),
        out_shape=jax.ShapeDtypeStruct((3 * cycles, NPHI), jnp.float32),
        compiler_params=pltpu.CompilerParams(vmem_limit_bytes=60 * 2**20),
    )(value, cycle, column)
    return out[:cycles] + out[cycles : 2 * cycles], out[2 * cycles :]


def local(scan_lines, response, cycle_offset, column, order_slot, legendre):
    filtered = noise_filter(scan_lines, response)
    band_cycles = legendre.shape[1]
    partial_value, counts = bin_samples(filtered, cycle_offset, column, band_cycles)
    summed, hit_total = side_by_side((partial_value, counts), "det", 0, 1)
    sky_map = summed / jnp.maximum(hit_total, 1.0)
    pixel_index = jnp.arange(NPHI, dtype=jnp.int32)[:, None]
    phases = 2.0 * jnp.pi / NPHI * (pixel_index * order_slot[None, :] % NPHI).astype(jnp.float32)
    cycle_real = jnp.dot(
        sky_map, jnp.cos(phases), precision=precise, preferred_element_type=jnp.float32
    )
    cycle_imag = -jnp.dot(
        sky_map, jnp.sin(phases), precision=precise, preferred_element_type=jnp.float32
    )
    cycle_modes = jnp.stack([cycle_real, cycle_imag])
    slot_count = legendre.shape[0]
    slot_start = lax.axis_index("det") * slot_count
    local_orders = lax.dynamic_slice_in_dim(order_slot, slot_start, slot_count, 0)
    degree_index = jnp.arange(LMAX, dtype=jnp.int32)
    keep_mask = (degree_index[None, :] >= local_orders[:, None]).astype(jnp.float32)
    terms = (
        jnp.einsum(
            "crs,srl->csl",
            lax.all_to_all(cycle_modes, "det", split_axis=2, concat_axis=1, tiled=True),
            legendre,
            precision=precise,
        )
        * keep_mask[None]
    )
    harmonics = summed_on_arrival(terms, "band", 2)
    return (harmonics, sky_map)


def solution(mesh):
    return jax.shard_map(
        local,
        mesh=mesh,
        in_specs=(
            P(("det", "band"), None),
            P(("det", "band"), None),
            P(("det", "band"), None),
            P(("det", "band"), None),
            P(),
            P("det", "band", None),
        ),
        out_specs=(P(None, "det", "band"), P(("band", "det"), None)),
        check_vma=False,
    )
```
